512 devices in a mesh: shot: 16 (over x_hi, z), space: 32 (over y, x_lo, core).
Axes of the slice: x: 4 (x_hi: 2, x_lo: 2; x = x_hi * 2 + x_lo), y: 8, z: 8, core: 2. Of those that a mesh axis runs over, the one named last changes fastest.
Arguments:
- courant: float32 [128, 256, 128], P('space'), may hold values from 0.02 to 0.18
- adjoint_now: float32 [16, 128, 256, 128], P('shot', 'space'), may hold values from -6 to 6
- adjoint_old: float32 [16, 128, 256, 128], P('shot', 'space'), may hold values from -6 to 6
- receiver_slab: int32 [16, 12288, 1], P('shot', 'space'), may hold values from 0 to 31; in each aligned block of 384 rows (0 to 383, 384 to 767, ..., all dimensions but the last counted through in order) at most 48 rows name the same one
- receiver_cell: int32 [16, 12288], P('shot', 'space'), may hold values from 0 to 131071
- residuals: float32 [16, 3, 12288], P('shot', None, 'space'), may hold values from -24 to 24
- forward_field: bfloat16 [16, 3, 128, 256, 128], P('shot', None, 'space'), may hold values from -6 to 6
Outputs:
- adjoint_last: float32 [16, 128, 256, 128], P('shot', 'space')
- adjoint_prior: float32 [16, 128, 256, 128], P('shot', 'space')
- gradient_image: float32 [128, 256, 128], P('space', 'shot')
The draws below stay inside these ranges and needn't reach their ends.
Inputs may be any that keep to these rules, and one draw needn't show every extreme that they name: `receiver_slab`: in each aligned block of 384 receivers (those held by one index of space) at most 48 lie in one slab, and some block reaches 48.
All inputs are finite; a program needn't handle non-finite values.
Results may differ from the reference program's by a relative error of at most 0.0003.
Values sent between devices are 32-bit elements; how exact they have to be, the bound alone decides.
No kernel may reach another device: no remote copies, remote signals or barrier semaphores. Data moves between devices by JAX's collectives and lax.ppermute only.
A program may use at most 64 MiB of HBM per device.

```python
import math
import jax
import jax.numpy as jnp
import numpy as np
from jax import lax

CX = 4
NY = 256
NZ = 128
STEPS = 3
REC_DEV = 384
CAP = 48
NX = 128
REC = 12288
SHOTS = 16
N_SPACE = 32


def place_ends(drawn, stream_key, smallest, largest):
    longest = drawn.shape.index(max(drawn.shape))
    spots = []
    for shift in (0, 1):
        where = [jax.random.randint(jax.random.fold_in(stream_key, axis), (), 0, length) for axis, length in enumerate(drawn.shape)]
        where[longest] = (where[longest] + shift) % drawn.shape[longest]
        spots.append(tuple(where))
    return drawn.at[spots[0]].set(smallest).at[spots[1]].set(largest)


def spiked(values, rng, source, target, shards_of, factor):
    def block_of(axis_at):
        return (jnp.arange(values.shape[axis_at]) // (values.shape[axis_at] // shards_of)).reshape((-1,) + (1,) * (values.ndim - 1 - axis_at))

    one_side = jax.random.permutation(rng, shards_of)[block_of(target)]
    second = (block_of(target) + shards_of // 2) % shards_of
    return jnp.where((block_of(source) == one_side) | (block_of(source) == second), factor * values, values)


def levels(key, shape, cuts, smallest, largest):
    def one(dim, shards_of):
        heights = jax.random.uniform(jax.random.fold_in(jax.random.fold_in(key, 6), dim), (shards_of,), jnp.float32, smallest / len(cuts), largest / len(cuts))
        return jnp.repeat(jnp.exp(heights), shape[dim] // shards_of).reshape((-1,) + (1,) * (len(shape) - dim - 1))

    level = one(*cuts[0])
    for cut in cuts[1:]:
        level = level * one(*cut)
    return level


def routed_block(key, own, number, rows, amount, top, most, lean):
    order = jax.random.permutation(key, amount)
    heavy_load, usual = shares(amount, rows * top, most, lean, True), shares(amount, rows * top, most, lean, False)
    places = jnp.arange(amount)

    def named(sizes, rotation):
        used = int((sizes > 0).sum())
        fixed = max(1, used // 4)
        passed = fixed + (places - fixed + rotation * (used - fixed)) % max(1, amount - fixed)
        return jnp.zeros((amount,), jnp.int32).at[order[jnp.where(places < fixed, places, passed)]].set(jnp.asarray(sizes, jnp.int32))

    sizes = jnp.where(number % 4 == 0, named(heavy_load, number // 4), named(usual, number - number // 4 - 1))
    mixed = jax.random.permutation(jax.random.fold_in(own, 3), amount)
    source_of, receiver = mixed[0:amount // 2 * 2:2], mixed[1:amount // 2 * 2:2]
    margin = jnp.minimum(sizes[source_of] - 1, most - sizes[receiver]) // 2
    margin = jnp.where((source_of == order[0]) | (receiver == order[0]) | (sizes[receiver] == 0), 0, jnp.maximum(margin, 0))
    passed = jax.random.randint(jax.random.fold_in(own, 4), (amount // 2,), 0, 1 << 20) % (margin + 1)
    sizes = sizes.at[source_of].add(-passed).at[receiver].add(passed)
    members = jnp.searchsorted(jnp.cumsum(sizes), jnp.arange(rows * top), side="right").astype(jnp.int32)
    listing = members.reshape(top, rows).T
    listing = listing[jax.random.permutation(jax.random.fold_in(own, 1), rows)]
    rotation = jax.random.randint(jax.random.fold_in(own, 2), (rows, 1), 0, top)
    return jnp.take_along_axis(listing, (jnp.arange(top)[None, :] + rotation) % top, axis=1)


def shares(amount, total, limit, lean, full):
    portions = [(1 << 20) // math.isqrt(standing ** lean) + 1 for standing in range(1, amount + 1)]
    largest = limit if full else min(limit, max(-(-total // amount), total * portions[0] // sum(portions)))
    least = 1 if total - largest >= amount - 1 else 0
    counts, spare = [largest] + [least] * (amount - 1), total - largest - least * (amount - 1)
    while spare > 0:
        movable = [i for i in range(1, amount) if counts[i] < largest] or [i for i in range(1, amount) if counts[i] < limit]
        mass, budget = sum([portions[i] for i in movable]), spare
        for i in movable:
            more = min(limit - counts[i], max(1, budget * portions[i] // mass), spare)
            counts[i] = counts[i] + more
            spare = spare - more
    return np.array(counts)


def bell_draw(rng, shape, spread, bound, shards=(), dtype=jnp.bfloat16):
    array = spread * jax.random.normal(rng, shape, jnp.float32)
    if shards:
        array = array * levels(rng, shape, shards, -0.22, 0.18)
    return jnp.clip(array, -bound, bound).astype(dtype)


def bell_draw_with(rng, extent, width, most, shards, heavy, held_as=jnp.bfloat16):
    drawn = width * jax.random.normal(rng, extent, jnp.float32)
    if shards:
        drawn = drawn * levels(rng, extent, shards, -0.22, 0.18)
    return jnp.clip(spiked(drawn, jax.random.fold_in(rng, 3), *heavy), -most, most).astype(held_as)


def setup_inputs(seed: int = 0) -> dict:
    arg_keys = jax.random.split(jax.random.key(seed), 8)
    courant = jnp.clip(jnp.exp(math.log(0.18) - 2.1972246 * jax.random.uniform(arg_keys[0], (NX, NY, NZ), jnp.float32) ** levels(arg_keys[0], (NX, NY, NZ), ((0, 32),), -0.2, 0.2)), 0.02, 0.18)
    adjoint_now = bell_draw(arg_keys[1], (SHOTS, NX, NY, NZ), 1.0, 6.0, ((0, 16), (1, 32)), jnp.float32)
    adjoint_old = bell_draw(arg_keys[2], (SHOTS, NX, NY, NZ), 1.0, 6.0, ((0, 16), (1, 32)), jnp.float32)
    receiver_slab_keys = jax.random.split(jax.random.fold_in(arg_keys[3], 1), SHOTS * REC // REC_DEV)
    receiver_slab_turns = jax.random.permutation(jax.random.fold_in(arg_keys[3], 3), SHOTS * REC // REC_DEV)
    receiver_slab = jax.vmap(lambda own, number: routed_block(jax.random.fold_in(arg_keys[3], 2), own, number, REC_DEV, N_SPACE, 1, CAP, 2))(receiver_slab_keys, receiver_slab_turns).reshape((SHOTS, REC, 1))
    receiver_cell = place_ends(jax.random.randint(arg_keys[4], (SHOTS, REC), 0, CX * NY * NZ), jax.random.fold_in(arg_keys[4], 1), 0, (CX * NY * NZ) - 1).astype(jnp.int32)
    residuals = bell_draw(arg_keys[5], (SHOTS, STEPS, REC), 4.0, 24.0, ((0, 16), (2, 32)), jnp.float32)
    forward_field = bell_draw_with(arg_keys[6], (SHOTS, STEPS, NX, NY, NZ), 1.0, 6.0, ((0, 16), (2, 32)), (0, 3, 16, 2.0))
    return {"courant": courant, "adjoint_now": adjoint_now, "adjoint_old": adjoint_old, "receiver_slab": receiver_slab, "receiver_cell": receiver_cell, "residuals": residuals, "forward_field": forward_field}


STENCIL_WEIGHTS = (-205.0 / 72.0, 8.0 / 5.0, -1.0 / 5.0, 8.0 / 315.0, -1.0 / 560.0)


def laplace(padded, extent_x, extent_y, extent_z):
    center = padded[4:4 + extent_x, 4:4 + extent_y, 4:4 + extent_z]
    summed = 3.0 * STENCIL_WEIGHTS[0] * center
    for offset in range(1, 5):
        along = padded[4 + offset:4 + offset + extent_x, 4:4 + extent_y, 4:4 + extent_z]
        along = along + padded[4 - offset:4 - offset + extent_x, 4:4 + extent_y, 4:4 + extent_z]
        along = along + padded[4:4 + extent_x, 4 + offset:4 + offset + extent_y, 4:4 + extent_z]
        along = along + padded[4:4 + extent_x, 4 - offset:4 - offset + extent_y, 4:4 + extent_z]
        along = along + padded[4:4 + extent_x, 4:4 + extent_y, 4 + offset:4 + offset + extent_z]
        along = along + padded[4:4 + extent_x, 4:4 + extent_y, 4 - offset:4 - offset + extent_z]
        summed = summed + STENCIL_WEIGHTS[offset] * along
    return summed


def reference(courant, adjoint_now, adjoint_old, receiver_slab, receiver_cell, residuals, forward_field):
    def one_shot(image_acc, inputs):
        current, previous, slab_ids, cell_ids, trace_rows, snapshots = inputs
        flat_cells = (slab_ids[:, 0] * (CX * NY * NZ) + cell_ids).astype(jnp.int32)
        for step_index in range(STEPS):
            source = jnp.zeros((NX * NY * NZ,), jnp.float32).at[flat_cells].add(trace_rows[step_index])
            source = source.reshape(NX, NY, NZ)
            padded = jnp.pad(current, 4)
            advanced = 2.0 * current - previous + courant * (laplace(padded, NX, NY, NZ) + source)
            image_acc = image_acc + snapshots[step_index].astype(jnp.float32) * advanced
            previous, current = current, advanced
        return image_acc, (current, previous)

    start = jnp.zeros((NX, NY, NZ), jnp.float32)
    image_sum, states = lax.scan(one_shot, start, (adjoint_now, adjoint_old, receiver_slab, receiver_cell, residuals, forward_field))
    return states[0], states[1], image_sum
```

```python
import jax
import jax.numpy as jnp
from jax import lax
from jax.experimental import pallas as pl
from jax.experimental.pallas import tpu as pltpu
from jax.sharding import PartitionSpec as P

STEPS = 3
CAP = 48
HALF = 64
LANES = 128
W = (-205.0 / 72.0, 8.0 / 5.0, -1.0 / 5.0, 8.0 / 315.0, -1.0 / 560.0)
F32 = jnp.float32
BF16 = jnp.bfloat16
VMEM = pl.BlockSpec(memory_space=pltpu.VMEM)
SMEM = pl.BlockSpec(memory_space=pltpu.SMEM)
NT = (((1,), (1,)), ((), ()))


def dot_nt(a, b):
    return lax.dot_general(a, b, NT, preferred_element_type=F32)


def parts(value, count):
    out = []
    for _ in range(count):
        head = value.astype(BF16)
        out.append(head.astype(F32))
        value = value - head.astype(F32)
    return out


def layer_of(par, k):
    return k + par * (3 - 2 * k)


def route_kernel(par_ref, slab_ref, cell_ref, res_ref, send_ref):
    rows = slab_ref.shape[1]
    slabs = send_ref.shape[0]
    slab = slab_ref[...]
    member = (slab == lax.broadcasted_iota(jnp.int32, (slabs, rows), 0)).astype(F32)
    earlier = (
        lax.broadcasted_iota(jnp.int32, (rows, rows), 0)
        < lax.broadcasted_iota(jnp.int32, (rows, rows), 1)
    ).astype(F32)
    before = jnp.dot(member.astype(BF16), earlier.astype(BF16), preferred_element_type=F32)
    rank = jnp.sum(before * member, axis=0, keepdims=True).astype(jnp.int32)
    spot = rank + HALF * par_ref[0]
    placed = spot == lax.broadcasted_iota(jnp.int32, (LANES, rows), 0)
    member = member.astype(BF16)
    for j in range(STEPS + 1):
        if j < STEPS:
            pieces = parts(res_ref[j], 2)
        else:
            pieces = parts(cell_ref[...].astype(F32), 3)
        total = None
        for piece in pieces:
            got = dot_nt(member, jnp.where(placed, piece, 0.0).astype(BF16))
            total = got if total is None else total + got
        send_ref[:, j, :] = total


def source_kernel(first, count, got_ref, *out_refs):
    pairs = got_ref.shape[0] // 2
    tiles = [got_ref[2 * m] + got_ref[2 * m + 1] for m in range(pairs)]
    cell = jnp.concatenate([tile[STEPS : STEPS + 1] for tile in tiles], axis=1).astype(jnp.int32)
    slots = cell.shape[1]
    row_count = out_refs[0].shape[0] * out_refs[0].shape[1]
    row, lane = cell // LANES, cell % LANES
    rows_hot = (row == lax.broadcasted_iota(jnp.int32, (row_count, slots), 0)).astype(F32).astype(BF16)
    lanes_hot = lane == lax.broadcasted_iota(jnp.int32, (LANES, slots), 0)
    for t in range(count):
        j = first + t
        value = jnp.concatenate([tile[j : j + 1] for tile in tiles], axis=1)
        high, low = parts(value, 2)
        right = jnp.concatenate(
            [jnp.where(lanes_hot, high, 0.0).astype(BF16), jnp.where(lanes_hot, low, 0.0).astype(BF16)],
            axis=0,
        )
        both = dot_nt(rows_hot, right)
        out_refs[t][...] = (both[:, :LANES] + both[:, LANES:]).reshape(out_refs[t].shape)


def base_kernel(par_ref, q_ref, old_ref, cour_ref, src_ref, near_ref, base_ref, pad_ref):
    par = par_ref[0]
    layers, rows, lanes = q_ref.shape
    edge = jnp.zeros((8, lanes), F32)
    for l in range(layers):
        pad_ref[l, 0:8, :] = edge
        pad_ref[l, 8 + rows : 16 + rows, :] = edge
        pad_ref[l, 8 : 8 + rows, :] = q_ref[l]
    spot = lax.broadcasted_iota(jnp.int32, (8, lanes), 1)
    step = 32
    for r in range(0, rows, step):
        own = [q_ref[layer_of(par, k), r : r + step, :] for k in range(layers)]
        near = [near_ref[layer_of(par, k), r : r + step, :] for k in range(layers)]
        stack = own + near
        for k in range(layers):
            at = layer_of(par, k)
            center = own[k]
            total = (3.0 * W[0]) * center
            for d in range(1, 5):
                along = stack[k + d]
                if k - d >= 0:
                    along = along + stack[k - d]
                along = along + pad_ref[at, 8 + r + d : 8 + r + d + step, :]
                along = along + pad_ref[at, 8 + r - d : 8 + r - d + step, :]
                total = total + W[d] * along
                up = jnp.where(spot < lanes - d, W[d], 0.0)
                down = jnp.where(spot >= d, W[d], 0.0)
                up = jnp.broadcast_to(up[None], (step // 8, 8, lanes)).reshape(step, lanes)
                down = jnp.broadcast_to(down[None], (step // 8, 8, lanes)).reshape(step, lanes)
                total = total + up * pltpu.roll(center, lanes - d, 1)
                total = total + down * pltpu.roll(center, d, 1)
            where = (at, pl.ds(r, step), slice(None))
            base_ref[where] = (
                2.0 * center - old_ref[where] + cour_ref[where] * (total + src_ref[where])
            )


def finish_kernel(t, par_ref, base_ref, cour_ref, far_ref, snap_ref, *refs):
    par = par_ref[0]
    layers, rows, lanes = base_ref.shape
    image_ref = refs[0] if t else None
    new_ref, out_ref = refs[-2:]
    step = 32
    for r in range(0, rows, step):
        far = [far_ref[layer_of(par, j), r : r + step, :] for j in range(layers)]
        for k in range(layers):
            at = layer_of(par, k)
            where = (at, pl.ds(r, step), slice(None))
            across = W[4] * far[k]
            for j in range(k + 1, layers):
                across = across + W[k + 4 - j] * far[j]
            new = base_ref[where] + cour_ref[where] * across
            new_ref[where] = new
            image = snap_ref[t, at, pl.ds(r, step), :].astype(F32) * new
            if t:
                image = image_ref[where] + image
            if t < STEPS - 1:
                out_ref[where] = image
            else:
                tall = out_ref.shape[2]
                for b in range(step // tall):
                    out_ref[r // tall + b, at] = image[b * tall : (b + 1) * tall]


def local(
    shots, courant, adjoint_now, adjoint_old, receiver_slab, receiver_cell, residuals, forward_field
):
    layers, rows, lanes = courant.shape
    spaces = lax.axis_size("space")
    field = jax.ShapeDtypeStruct((layers, rows, lanes), F32)
    par = (lax.axis_index("space") % 2).astype(jnp.int32).reshape(1)
    near_pairs = [(i, i ^ 1) for i in range(spaces)]
    far_pairs = [(i, i + 1) for i in range(1, spaces - 1, 2)]
    far_pairs = far_pairs + [(b, a) for a, b in far_pairs]

    current, previous = adjoint_now[0], adjoint_old[0]
    snaps = forward_field[0]
    slab = receiver_slab.reshape(1, -1)
    values = jnp.transpose(residuals, (1, 0, 2))
    send = pl.pallas_call(
        route_kernel,
        out_shape=jax.ShapeDtypeStruct((spaces, STEPS + 1, LANES), F32),
        in_specs=[SMEM, VMEM, VMEM, VMEM],
        out_specs=VMEM,
        name="route",
    )(par, slab, receiver_cell, values)
    got = lax.all_to_all(send, "space", split_axis=0, concat_axis=0, tiled=True)

    def sources(first, count):
        def body(*refs):
            source_kernel(first, count, *refs)

        return pl.pallas_call(
            body,
            out_shape=[field] * count,
            in_specs=[VMEM],
            out_specs=[VMEM] * count,
            name=f"sources_{first}",
        )(got)

    image = None
    source = sources(0, 1)
    for t in range(STEPS):
        far = lax.ppermute(current, "space", far_pairs)
        near = lax.ppermute(current, "space", near_pairs)
        base = pl.pallas_call(
            base_kernel,
            out_shape=field,
            in_specs=[SMEM] + [VMEM] * 5,
            out_specs=VMEM,
            scratch_shapes=[pltpu.VMEM((layers, rows + 16, lanes), F32)],
            name=f"base_{t}",
        )(par, current, previous, courant, source[t], near)
        if t == 0:
            source = source + sources(1, STEPS - 1)

        def finish(*refs, t=t):
            finish_kernel(t, *refs)

        last = t == STEPS - 1
        shape = field
        if last:
            shape = jax.ShapeDtypeStruct((shots, layers, rows // shots, lanes), F32)
        carried = [image] if t else []
        advanced, image = pl.pallas_call(
            finish,
            out_shape=[field, shape],
            in_specs=[SMEM] + [VMEM] * (4 + len(carried)),
            out_specs=[VMEM, VMEM],
            name=f"finish_{t}",
        )(par, base, courant, far, snaps, *carried)
        previous, current = current, advanced
    arrived = lax.all_to_all(image, "shot", split_axis=0, concat_axis=0, tiled=True)
    return (current[None], previous[None], arrived.sum(axis=0))


def solution(mesh):
    shots = mesh.shape["shot"]
    in_specs = (
        P("space", None, None),
        P("shot", "space", None, None),
        P("shot", "space", None, None),
        P("shot", "space", None),
        P("shot", "space"),
        P("shot", None, "space"),
        P("shot", None, "space", None, None),
    )
    out_specs = (
        P("shot", "space", None, None),
        P("shot", "space", None, None),
        P("space", "shot", None),
    )

    def body(*args):
        return local(shots, *args)

    return jax.shard_map(body, mesh=mesh, in_specs=in_specs, out_specs=out_specs, check_vma=False)
```
